256 devices in a mesh: grid: 8 (over y, core), wide: 32 (over z, x).
Axes of the slice: x: 4, y: 4, z: 8, core: 2. Of those that a mesh axis runs over, the one named last changes fastest.
Arguments:
- values: bfloat16 [3584, 64, 4096], P(('grid', 'wide')), may hold values from 0 to 1
- a_block: int32 [3584], P(('grid', 'wide')), may hold values from 0 to 63, as said below
- b_block: int32 [3584], P(('grid', 'wide')), may hold values from 0 to 15
- c_block: int32 [3584], P(('grid', 'wide')), may hold values from 0 to 63
- held: int32 [3584], P(('grid', 'wide')), may hold values from 0 to 1, as said below
- factor_a: bfloat16 [32768, 256], P(('grid', 'wide')), may hold values from -6 to 6
- factor_b: bfloat16 [32768, 256], P(('wide', 'grid')), may hold values from -2.390625 to 2.390625
- factor_c: bfloat16 [4096, 256], replicated, may hold values from -2.390625 to 2.390625
Outputs:
- next_a: float32 [32768, 256], P(('grid', 'wide'))
- next_b: float32 [32768, 256], P(('wide', 'grid'))
- held_loss: float32 [], replicated
The draws below stay inside these ranges and needn't reach their ends.
Inputs may be any that keep to these rules, and one draw needn't show every extreme that they name: Among the blocks of one device, at most 1 have a_block values with the same a_block // 2; on some device some such value is shared by exactly 1 block. Every device holds 1 to 3 held-out blocks; some device holds exactly 3.
All inputs are finite; a program needn't handle non-finite values.
Results may differ from the reference program's by a relative error of at most 0.0011.
Values may be sent and summed in bfloat16 or wider, within the bound.
No kernel may reach another device: no remote copies, remote signals or barrier semaphores. Data moves between devices by JAX's collectives and lax.ppermute only.
A program may use at most 64 MiB of HBM per device.

```python
import jax
import jax.numpy as jnp
from jax import lax

R = 256
BS = 64
NB_DEV = 14
A_ROWS_DEV = 128
K = 4096
HELD_MAX = 3
BLOCKS = 3584
I_ROWS = 32768
J_ROWS = 32768
A_PBLK = 64
B_PBLK = 16
CAP = 1
N_WIDE = 32


def draw_a_block(key, part):
    devices = BLOCKS // NB_DEV
    per_holder = A_ROWS_DEV // BS
    keys = jax.random.split(key, devices)

    def single(sub_key):
        first_key, second_key = jax.random.split(sub_key)
        pool = jnp.arange(CAP * N_WIDE, dtype=jnp.int32) % N_WIDE
        holders = jax.random.permutation(first_key, pool)[:NB_DEV]
        within = jax.random.randint(second_key, (NB_DEV,), 0, per_holder, dtype=jnp.int32)
        return (holders, within)
    holders, within = jax.vmap(single)(keys)
    shifted = (holders[0] - holders[0, 0] + N_WIDE - 1) % N_WIDE
    holders = holders.at[0].set(shifted)
    within = within.at[0, 0].set(per_holder - 1)
    return (holders * per_holder + within).reshape(-1).astype(jnp.int32)


def draw_held(key, part):
    devices = BLOCKS // NB_DEV
    count_key, order_key = jax.random.split(jax.random.fold_in(key, 7))
    counts = jax.random.randint(count_key, (devices,), 1, HELD_MAX + 1, dtype=jnp.int32)
    counts = counts.at[0].set(HELD_MAX)
    orders = jax.vmap(lambda sub_key: jax.random.permutation(sub_key, NB_DEV))(jax.random.split(order_key, devices))
    return (orders < counts[:, None]).astype(jnp.int32).reshape(-1)


def draw_factor_a(key, part):
    sub_key = jax.random.fold_in(key, 11)
    fraction = jnp.arange(I_ROWS, dtype=jnp.float32) / (I_ROWS - 1.0)
    spread = 0.12 * jnp.exp(fraction * jnp.log(20.0))
    noise = jnp.clip(jax.random.normal(sub_key, (I_ROWS, R), jnp.float32), -2.4, 2.4)
    return (noise * spread[:, None]).astype(jnp.bfloat16)


def plant(result, own_key, low, largest):
    longest = result.shape.index(max(result.shape))
    spots = []
    for shift in (0, 1):
        where = [jax.random.randint(jax.random.fold_in(own_key, axis), (), 0, length) for axis, length in enumerate(result.shape)]
        where[longest] = (where[longest] + shift) % result.shape[longest]
        spots.append(tuple(where))
    return result.at[spots[0]].set(low).at[spots[1]].set(largest)


def block_scale(rng, extent, pieces, smallest, largest):
    level, own = 1.0, jax.random.fold_in(rng, 6)
    for position, blocks in pieces:
        steps = jnp.exp(jax.random.uniform(jax.random.fold_in(own, position), (blocks,), jnp.float32, smallest / len(pieces), largest / len(pieces)))
        level = level * jnp.repeat(steps, extent[position] // blocks).reshape([-1 if axis == position else 1 for axis in range(len(extent))])
    return level


def gaussian(stream_key, extent, scale, limit, cuts=(), kind=jnp.bfloat16):
    factor_of = block_scale(stream_key, extent, cuts, -0.22, 0.18) if cuts else 1.0
    values = jax.random.normal(stream_key, extent, jnp.float32) * scale * factor_of
    return jnp.minimum(jnp.maximum(values, -limit), limit).astype(kind)


def setup_inputs(seed: int = 0) -> dict:
    key_of = jax.random.split(jax.random.key(seed), 9)
    values = jnp.clip(1.0 * jax.random.uniform(key_of[0], (BLOCKS, BS, BS * BS), jnp.float32) ** block_scale(key_of[0], (BLOCKS, BS, BS * BS), ((0, 256),), -0.2, 0.2), 0.0, 1.0).astype(jnp.bfloat16)
    a_block = draw_a_block(jax.random.fold_in(key_of[8], 71), 0)
    b_block = plant(jax.random.randint(key_of[2], (BLOCKS,), 0, B_PBLK), jax.random.fold_in(key_of[2], 1), 0, B_PBLK - 1).astype(jnp.int32)
    c_block = plant(jax.random.randint(key_of[3], (BLOCKS,), 0, K // BS), jax.random.fold_in(key_of[3], 1), 0, (K // BS) - 1).astype(jnp.int32)
    held = draw_held(jax.random.fold_in(key_of[8], 71), 0)
    factor_a = draw_factor_a(jax.random.fold_in(key_of[8], 71), 0)
    factor_b = gaussian(key_of[6], (J_ROWS, R), 0.4, 2.390625, ((0, 256),))
    factor_c = gaussian(key_of[7], (K, R), 0.4, 2.390625)
    return {"values": values, "a_block": a_block, "b_block": b_block, "c_block": c_block, "held": held, "factor_a": factor_a, "factor_b": factor_b, "factor_c": factor_c}


step_size = 0.05


def reference(values, a_block, b_block, c_block, held, factor_a, factor_b, factor_c):
    devices = BLOCKS // NB_DEV
    a_blocks = factor_a.reshape(I_ROWS // BS, BS, R)
    b_blocks = factor_b.reshape(J_ROWS // BS, BS, R)
    c_blocks = factor_c.reshape(K // BS, BS, R)
    highest = lax.Precision.HIGHEST

    def visit(carry, device):
        grad_a, grad_b, loss_total, held_total = carry
        start = device * NB_DEV
        entries = lax.dynamic_slice_in_dim(values, start, NB_DEV, 0).astype(jnp.float32)
        a_index = (device // N_WIDE) * A_PBLK + lax.dynamic_slice_in_dim(a_block, start, NB_DEV, 0)
        b_index = (device % N_WIDE) * B_PBLK + lax.dynamic_slice_in_dim(b_block, start, NB_DEV, 0)
        c_index = lax.dynamic_slice_in_dim(c_block, start, NB_DEV, 0)
        flags = lax.dynamic_slice_in_dim(held, start, NB_DEV, 0).astype(jnp.float32)
        a_rows = a_blocks[a_index].astype(jnp.float32)
        b_rows = b_blocks[b_index].astype(jnp.float32)
        c_rows = c_blocks[c_index].astype(jnp.float32)
        khatri = (b_rows[:, :, None, :] * c_rows[:, None, :, :]).astype(jnp.bfloat16)
        khatri = lax.optimization_barrier(khatri).astype(jnp.float32).reshape(NB_DEV, BS * BS, R)
        model = jnp.einsum("nar,nkr->nak", a_rows, khatri, precision=highest)
        weight = flags[:, None, None]
        resid = ((jax.nn.sigmoid(model) - entries) * (1.0 - weight)).astype(jnp.bfloat16)
        resid = lax.optimization_barrier(resid).astype(jnp.float32)
        loss_total = loss_total + jnp.sum((jax.nn.softplus(model) - entries * model) * weight)
        grad_rows = jnp.einsum("nak,nkr->nar", resid, khatri, precision=highest)
        partial_sum = jnp.einsum("nak,nar->nkr", resid, a_rows, precision=highest).reshape(NB_DEV, BS, BS, R)
        grad_cols = jnp.sum(partial_sum * c_rows[:, None, :, :], axis=2)
        grad_a = grad_a.at[a_index].add(grad_rows)
        grad_b = grad_b.at[b_index].add(grad_cols)
        return (grad_a, grad_b, loss_total, held_total + jnp.sum(flags)), None

    start_carry = (jnp.zeros((I_ROWS // BS, BS, R), jnp.float32), jnp.zeros((J_ROWS // BS, BS, R), jnp.float32),
                   jnp.zeros((), jnp.float32), jnp.zeros((), jnp.float32))
    final, unused = lax.scan(visit, start_carry, jnp.arange(devices, dtype=jnp.int32))
    grad_a, grad_b, loss_total, held_total = final
    next_a = factor_a.astype(jnp.float32) - step_size * grad_a.reshape(I_ROWS, R)
    next_b = factor_b.astype(jnp.float32) - step_size * grad_b.reshape(J_ROWS, R)
    held_loss = loss_total / (held_total * (BS * BS * BS))
    return next_a, next_b, held_loss
```

```python
import jax
import jax.numpy as jnp
from jax import lax
from jax.experimental import pallas as pl
from jax.experimental.pallas import tpu as pltpu
from jax.sharding import Mesh, PartitionSpec as P

step_size = 0.05
f32 = jnp.float32
bf16 = jnp.bfloat16
GROUP = 8


def block_kernel(
    tab, values_ref, a_ref, b_ref, c_ref, slots_ref, b_grad_ref, loss_ref
):
    i = pl.program_id(0)

    @pl.when(i == 0)
    def _():
        slots_ref[...] = jnp.zeros_like(slots_ref)
        b_grad_ref[...] = jnp.zeros_like(b_grad_ref)
        loss_ref[...] = jnp.zeros_like(loss_ref)

    a_rows = a_ref[0]
    c_rows = c_ref[0]
    side, width = a_rows.shape
    held = tab[3, i]
    span = GROUP * side

    def khatri_of(group):
        b_rows = b_ref[0, pl.ds(group * GROUP, GROUP), :]
        product = b_rows.astype(f32)[:, None, :] * c_rows.astype(f32)[None, :, :]
        return product.astype(bf16).reshape(span, width)

    def model_of(khatri):
        return lax.dot_general(
            a_rows, khatri, (((1,), (1,)), ((), ())), preferred_element_type=f32
        )

    @pl.when(held == 0)
    def _():
        c_f = c_rows.astype(f32)
        b_index = tab[1, i]
        slot = tab[4, i]
        grad_rows = jnp.zeros((side, width), f32)
        for group in range(side // GROUP):
            khatri = khatri_of(group)
            model = model_of(khatri)
            entries = values_ref[0, :, group * span : (group + 1) * span].astype(f32)
            sigmoid = 0.5 * jnp.tanh(0.5 * model) + 0.5
            resid = (sigmoid - entries).astype(bf16)
            grad_rows = grad_rows + jnp.dot(resid, khatri, preferred_element_type=f32)
            partial_sum = lax.dot_general(
                resid, a_rows, (((0,), (0,)), ((), ())), preferred_element_type=f32
            )
            cols = jnp.sum(partial_sum.reshape(GROUP, side, width) * c_f[None], axis=1)
            at = (b_index, pl.ds(group * GROUP, GROUP), slice(None))
            b_grad_ref[at] = b_grad_ref[at] + cols
        slots_ref[slot, pl.ds(0, side), :] = grad_rows
        slots_ref[slot, pl.ds(side, 8), :] = jnp.full((8, width), tab[5, i].astype(f32), f32)

    @pl.when(held != 0)
    def _():
        total = jnp.zeros((side, span), f32)
        for group in range(side // GROUP):
            model = model_of(khatri_of(group))
            entries = values_ref[0, :, group * span : (group + 1) * span].astype(f32)
            soft = jnp.maximum(model, 0.0) + jnp.log1p(jnp.exp(-jnp.abs(model)))
            total = total + (soft - entries * model)
        folded = total.reshape(side // 8, 8, span).sum(axis=0)
        lanes = folded[:, 0:128]
        for k in range(1, span // 128):
            lanes = lanes + folded[:, k * 128 : (k + 1) * 128]
        loss_ref[...] = loss_ref[...] + lanes


def run_blocks(table, values, a_panel, b_panel, c_panel, n_slots):
    side, width = a_panel.shape[1:]
    whole3 = lambda i, tab: (0, 0, 0)
    grid_spec = pltpu.PrefetchScalarGridSpec(
        num_scalar_prefetch=1,
        grid=(values.shape[0],),
        in_specs=[
            pl.BlockSpec((1,) + values.shape[1:], lambda i, tab: (i, 0, 0)),
            pl.BlockSpec((1, side, width), lambda i, tab: (tab[0, i], 0, 0)),
            pl.BlockSpec((1, side, width), lambda i, tab: (tab[1, i], 0, 0)),
            pl.BlockSpec((1, side, width), lambda i, tab: (tab[2, i], 0, 0)),
        ],
        out_specs=[
            pl.BlockSpec((n_slots, side + 8, width), whole3),
            pl.BlockSpec(b_panel.shape, whole3),
            pl.BlockSpec((8, 128), lambda i, tab: (0, 0)),
        ],
    )
    return pl.pallas_call(
        block_kernel,
        out_shape=[
            jax.ShapeDtypeStruct((n_slots, side + 8, width), f32),
            jax.ShapeDtypeStruct(b_panel.shape, f32),
            jax.ShapeDtypeStruct((8, 128), f32),
        ],
        grid_spec=grid_spec,
    )(table, values, a_panel, b_panel, c_panel)


def step(values, a_block, b_block, c_block, held, factor_a, factor_b, factor_c):
    side, width = values.shape[1], factor_a.shape[1]
    nz, nx = lax.axis_size("z"), lax.axis_size("x")
    grid_axes, wide_axes = ("y", "core"), ("z", "x")
    n_grid, n_wide = lax.axis_size(grid_axes), nz * nx
    z, x = lax.axis_index("z"), lax.axis_index("x")
    own = factor_a.shape[0] // side

    def shift(v, axis, by):
        n = lax.axis_size(axis)
        return lax.ppermute(v, axis, [(k, (k + by) % n) for k in range(n)])

    column = jnp.concatenate([factor_a] + [shift(factor_a, "z", s) for s in range(1, nz)])
    b_panel = lax.all_gather(factor_b, grid_axes, axis=0, tiled=True).reshape(-1, side, width)
    half = column.shape[0] // 2
    ahead = shift(column, "x", 1)
    back = shift(column, "x", nx - 1)
    far = [shift(ahead[:half], "x", 1), shift(back[half:], "x", nx - 1)]
    a_panel = jnp.concatenate([column, ahead, *far, back]).reshape(-1, side, width)
    c_panel = factor_c.reshape(-1, side, width)

    holder = a_block // own
    within = a_block % own
    s = (z - holder // nx) % nz
    q = (x - holder % nx) % nx
    table = jnp.stack([(q * nz + s) * own + within, b_block, c_block, held, holder, within])
    slots, b_grad, loss = run_blocks(table, values, a_panel, b_panel, c_panel, n_wide)

    totals = jnp.stack([jnp.sum(loss), jnp.sum(held).astype(f32)])
    extra = jnp.broadcast_to(totals[None, :, None], (n_grid, 2, width))
    extra = jnp.concatenate([extra, jnp.zeros((n_grid, 6, width), f32)], axis=1)
    sent = jnp.concatenate([b_grad.reshape(n_grid, -1, width), extra], axis=1)
    got = jnp.sum(lax.all_to_all(sent, grid_axes, 0, 0, tiled=True), axis=0)
    rows = factor_b.shape[0]
    grad_b = got[:rows]
    group_totals = jnp.broadcast_to(got[None, rows : rows + 2], (n_wide, 2, width))
    sent = lax.dynamic_update_slice(slots, group_totals, (0, side + 1, 0))
    got = lax.all_to_all(sent, wide_axes, 0, 0, tiled=True)
    which = got[:, side : side + 1, :1]
    grad_a = jnp.concatenate(
        [jnp.sum(jnp.where(which == k, got[:, :side], 0.0), axis=0) for k in range(own)]
    )
    totals = jnp.sum(got[:, side + 1 : side + 3, 0], axis=0)
    held_loss = totals[0] / (totals[1] * (side * side * side))
    next_a = factor_a.astype(f32) - step_size * grad_a
    next_b = factor_b.astype(f32) - step_size * grad_b
    return next_a, next_b, held_loss


def solution(mesh):
    fine = Mesh(mesh.devices.reshape(4, 2, 8, 4), ("y", "core", "z", "x"))
    blocks = ("y", "core", "z", "x")
    rows_b = ("z", "x", "y", "core")
    in_specs = (
        P(blocks, None, None), P(blocks), P(blocks), P(blocks), P(blocks),
        P(blocks, None), P(rows_b, None), P(),
    )
    out_specs = (P(blocks, None), P(rows_b, None), P())
    return jax.shard_map(step, mesh=fine, in_specs=in_specs, out_specs=out_specs, check_vma=False)
```

```python
import jax
import jax.numpy as jnp
from jax import lax
from jax.experimental import pallas as pl
from jax.experimental.pallas import tpu as pltpu
from jax.sharding import Mesh, PartitionSpec as P

step_size = 0.05
f32 = jnp.float32
bf16 = jnp.bfloat16
f16 = jnp.float16
LANES = 128
HEAD = 16
TOP = 14
GROUP = 8


def power_of(size):
    return jnp.ceil(jnp.log(jnp.maximum(size, 1e-30)) * (1.0 / 0.6931471805599453))


def block_kernel(
    tab, values_ref, a_ref, b_ref, c_ref, slots_ref, b_grad_ref, loss_ref
):
    i = pl.program_id(0)

    @pl.when(i == 0)
    def _():
        slots_ref[...] = jnp.zeros_like(slots_ref)
        b_grad_ref[...] = jnp.zeros_like(b_grad_ref)
        loss_ref[...] = jnp.zeros_like(loss_ref)

    a_rows = a_ref[0]
    c_rows = c_ref[0]
    side, width = a_rows.shape
    held = tab[3, i]
    span = GROUP * side

    def khatri_of(group):
        b_rows = b_ref[0, pl.ds(group * GROUP, GROUP), :]
        product = b_rows.astype(f32)[:, None, :] * c_rows.astype(f32)[None, :, :]
        return product.astype(bf16).reshape(span, width)

    def model_of(khatri):
        return lax.dot_general(
            a_rows, khatri, (((1,), (1,)), ((), ())), preferred_element_type=f32
        )

    @pl.when(held == 0)
    def _():
        c_f = c_rows.astype(f32)
        b_index = tab[1, i]
        slot = tab[4, i]
        grad_rows = jnp.zeros((side, width), f32)
        for group in range(side // GROUP):
            khatri = khatri_of(group)
            model = model_of(khatri)
            entries = values_ref[0, :, group * span : (group + 1) * span].astype(f32)
            sigmoid = 0.5 * jnp.tanh(0.5 * model) + 0.5
            resid = (sigmoid - entries).astype(bf16)
            grad_rows = grad_rows + jnp.dot(resid, khatri, preferred_element_type=f32)
            partial_sum = lax.dot_general(
                resid, a_rows, (((0,), (0,)), ((), ())), preferred_element_type=f32
            )
            cols = jnp.sum(partial_sum.reshape(GROUP, side, width) * c_f[None], axis=1)
            at = (b_index, pl.ds(group * GROUP, GROUP), slice(None))
            b_grad_ref[at] = b_grad_ref[at] + cols
        power = power_of(jnp.max(jnp.abs(grad_rows), axis=(0, 1), keepdims=True))
        scaled = (grad_rows * jnp.exp2(TOP - power)).astype(slots_ref.dtype)
        for part in range(width // LANES):
            columns = slice(part * LANES, (part + 1) * LANES)
            slots_ref[slot, pl.ds(part * side, side), :] = scaled[:, columns]
        row = lax.broadcasted_iota(jnp.int32, (HEAD, LANES), 0)
        head = jnp.where(row == 0, tab[5, i].astype(f32), jnp.where(row == 1, power, 0.0))
        slots_ref[slot, pl.ds(side * width // LANES, HEAD), :] = head.astype(slots_ref.dtype)

    @pl.when(held != 0)
    def _():
        total = jnp.zeros((side, span), f32)
        for group in range(side // GROUP):
            model = model_of(khatri_of(group))
            entries = values_ref[0, :, group * span : (group + 1) * span].astype(f32)
            soft = jnp.maximum(model, 0.0) + jnp.log1p(jnp.exp(-jnp.abs(model)))
            total = total + (soft - entries * model)
        folded = total.reshape(side // 8, 8, span).sum(axis=0)
        lanes = folded[:, 0:128]
        for k in range(1, span // 128):
            lanes = lanes + folded[:, k * 128 : (k + 1) * 128]
        loss_ref[...] = loss_ref[...] + lanes


def run_blocks(table, values, a_panel, b_panel, c_panel, n_slots):
    side, width = a_panel.shape[1:]
    whole3 = lambda i, tab: (0, 0, 0)
    grid_spec = pltpu.PrefetchScalarGridSpec(
        num_scalar_prefetch=1,
        grid=(values.shape[0],),
        in_specs=[
            pl.BlockSpec((1,) + values.shape[1:], lambda i, tab: (i, 0, 0)),
            pl.BlockSpec((1, side, width), lambda i, tab: (tab[0, i], 0, 0)),
            pl.BlockSpec((1, side, width), lambda i, tab: (tab[1, i], 0, 0)),
            pl.BlockSpec((1, side, width), lambda i, tab: (tab[2, i], 0, 0)),
        ],
        out_specs=[
            pl.BlockSpec((n_slots, side * width // LANES + HEAD, LANES), whole3),
            pl.BlockSpec(b_panel.shape, whole3),
            pl.BlockSpec((8, 128), lambda i, tab: (0, 0)),
        ],
    )
    return pl.pallas_call(
        block_kernel,
        out_shape=[
            jax.ShapeDtypeStruct((n_slots, side * width // LANES + HEAD, LANES), f32),
            jax.ShapeDtypeStruct(b_panel.shape, f32),
            jax.ShapeDtypeStruct((8, 128), f32),
        ],
        grid_spec=grid_spec,
    )(table, values, a_panel, b_panel, c_panel)


def step(values, a_block, b_block, c_block, held, factor_a, factor_b, factor_c):
    side, width = values.shape[1], factor_a.shape[1]
    nz, nx = lax.axis_size("z"), lax.axis_size("x")
    grid_axes, wide_axes = ("y", "core"), ("z", "x")
    n_grid, n_wide = lax.axis_size(grid_axes), nz * nx
    z, x = lax.axis_index("z"), lax.axis_index("x")
    own = factor_a.shape[0] // side

    def shift(v, axis, by):
        n = lax.axis_size(axis)
        return lax.ppermute(v, axis, [(k, (k + by) % n) for k in range(n)])

    column = jnp.concatenate([factor_a] + [shift(factor_a, "z", s) for s in range(1, nz)])
    b_panel = lax.all_gather(factor_b, grid_axes, axis=0, tiled=True).reshape(-1, side, width)
    half = column.shape[0] // 2
    ahead = shift(column, "x", 1)
    back = shift(column, "x", nx - 1)
    far = [shift(ahead[:half], "x", 1), shift(back[half:], "x", nx - 1)]
    a_panel = jnp.concatenate([column, ahead, *far, back]).reshape(-1, side, width)
    c_panel = factor_c.reshape(-1, side, width)

    holder = a_block // own
    within = a_block % own
    s = (z - holder // nx) % nz
    q = (x - holder % nx) % nx
    table = jnp.stack([(q * nz + s) * own + within, b_block, c_block, held, holder, within])
    slots, b_grad, loss = run_blocks(table, values, a_panel, b_panel, c_panel, n_wide)

    totals = jnp.stack([jnp.sum(loss), jnp.sum(held).astype(f32)])
    extra = jnp.broadcast_to(totals[None, :, None], (n_grid, 2, width))
    extra = jnp.concatenate([extra, jnp.zeros((n_grid, 6, width), f32)], axis=1)
    sent = jnp.concatenate([b_grad.reshape(n_grid, -1, width), extra], axis=1)
    got = jnp.sum(lax.all_to_all(sent, grid_axes, 0, 0, tiled=True), axis=0)
    rows = factor_b.shape[0]
    grad_b = got[:rows]
    loss_group, held_group = got[rows, 0], got[rows + 1, 0]
    loss_power = power_of(jnp.abs(loss_group))
    fraction = loss_group * jnp.exp2(-loss_power)
    lead = lax.reduce_precision(fraction, 5, 10)
    rest = (fraction - lead) * 2048.0
    head = jnp.stack([loss_power, lead, rest, held_group]).astype(f16)
    head = jnp.broadcast_to(head[None, :, None], (n_wide, 4, LANES))
    tall = side * width // LANES
    sent = lax.dynamic_update_slice(slots.astype(f16), head, (0, tall + 2, 0))
    got = lax.all_to_all(sent, wide_axes, 0, 0, tiled=True)
    heads = got[:, tall : tall + 6, 0].astype(f32)
    which, scale = heads[:, 0], jnp.exp2(heads[:, 1] - TOP)
    picked = jnp.where(which[None, :] == jnp.arange(own, dtype=f32)[:, None], scale[None, :], 0.0)
    grads = got[:, :tall].astype(f32)
    grad_a = jnp.stack([jnp.sum(picked[k][:, None, None] * grads, axis=0) for k in range(own)])
    grad_a = grad_a.reshape(own, width // LANES, side, LANES).transpose(0, 2, 1, 3)
    grad_a = grad_a.reshape(own * side, width)
    totals = [
        jnp.sum(jnp.exp2(heads[:, 2]) * (heads[:, 3] + heads[:, 4] / 2048.0)),
        jnp.sum(heads[:, 5]),
    ]
    held_loss = totals[0] / (totals[1] * (side * side * side))
    next_a = factor_a.astype(f32) - step_size * grad_a
    next_b = factor_b.astype(f32) - step_size * grad_b
    return next_a, next_b, held_loss


def solution(mesh):
    fine = Mesh(mesh.devices.reshape(4, 2, 8, 4), ("y", "core", "z", "x"))
    blocks = ("y", "core", "z", "x")
    rows_b = ("z", "x", "y", "core")
    in_specs = (
        P(blocks, None, None), P(blocks), P(blocks), P(blocks), P(blocks),
        P(blocks, None), P(rows_b, None), P(),
    )
    out_specs = (P(blocks, None), P(rows_b, None), P())
    return jax.shard_map(step, mesh=fine, in_specs=in_specs, out_specs=out_specs, check_vma=False)
```

```python
import jax
import jax.numpy as jnp
from jax import lax
from jax.experimental import pallas as pl
from jax.experimental.pallas import tpu as pltpu
from jax.sharding import Mesh, PartitionSpec as P

step_size = 0.05
f32 = jnp.float32
bf16 = jnp.bfloat16
f16 = jnp.float16
LANES = 128
HEAD = 16
TOP = 14
GROUP = 8


def power_of(size):
    return jnp.ceil(jnp.log(jnp.maximum(size, 1e-30)) * (1.0 / 0.6931471805599453))


def block_kernel(
    tab, values_ref, a_ref, b_ref, c_ref, slots_ref, b_grad_ref, loss_ref
):
    i = pl.program_id(0)

    @pl.when(i == 0)
    def _():
        slots_ref[...] = jnp.zeros_like(slots_ref)
        b_grad_ref[...] = jnp.zeros_like(b_grad_ref)
        loss_ref[...] = jnp.zeros_like(loss_ref)

    a_rows = a_ref[0]
    c_rows = c_ref[0]
    side, width = a_rows.shape
    held = tab[3, i]
    span = GROUP * side

    def khatri_of(group):
        b_rows = b_ref[0, pl.ds(group * GROUP, GROUP), :]
        product = b_rows.astype(f32)[:, None, :] * c_rows.astype(f32)[None, :, :]
        return product.astype(bf16).reshape(span, width)

    def model_of(khatri):
        return lax.dot_general(
            a_rows, khatri, (((1,), (1,)), ((), ())), preferred_element_type=f32
        )

    @pl.when(held == 0)
    def _():
        c_f = c_rows.astype(f32)
        b_index = tab[1, i]
        slot = tab[4, i]
        grad_rows = jnp.zeros((side, width), f32)
        for group in range(side // GROUP):
            khatri = khatri_of(group)
            model = model_of(khatri)
            entries = values_ref[0, :, group * span : (group + 1) * span].astype(f32)
            sigmoid = 0.5 * jnp.tanh(0.5 * model) + 0.5
            resid = (sigmoid - entries).astype(bf16)
            grad_rows = grad_rows + jnp.dot(resid, khatri, preferred_element_type=f32)
            partial_sum = lax.dot_general(
                resid, a_rows, (((0,), (0,)), ((), ())), preferred_element_type=f32
            )
            cols = jnp.sum(partial_sum.reshape(GROUP, side, width) * c_f[None], axis=1)
            at = (b_index, pl.ds(group * GROUP, GROUP), slice(None))
            b_grad_ref[at] = b_grad_ref[at] + cols
        power = power_of(jnp.max(jnp.abs(grad_rows), axis=(0, 1), keepdims=True))
        scaled = (grad_rows * jnp.exp2(TOP - power)).astype(slots_ref.dtype)
        for part in range(width // LANES):
            columns = slice(part * LANES, (part + 1) * LANES)
            slots_ref[slot, pl.ds(part * side, side), :] = scaled[:, columns]
        row = lax.broadcasted_iota(jnp.int32, (HEAD, LANES), 0)
        head = jnp.where(row == 0, tab[5, i].astype(f32), jnp.where(row == 1, power, 0.0))
        slots_ref[slot, pl.ds(side * width // LANES, HEAD), :] = head.astype(slots_ref.dtype)

    @pl.when(held != 0)
    def _():
        total = jnp.zeros((side, span), f32)
        for group in range(side // GROUP):
            model = model_of(khatri_of(group))
            entries = values_ref[0, :, group * span : (group + 1) * span].astype(f32)
            soft = jnp.maximum(model, 0.0) + jnp.log1p(jnp.exp(-jnp.abs(model)))
            total = total + (soft - entries * model)
        folded = total.reshape(side // 8, 8, span).sum(axis=0)
        lanes = folded[:, 0:128]
        for k in range(1, span // 128):
            lanes = lanes + folded[:, k * 128 : (k + 1) * 128]
        loss_ref[...] = loss_ref[...] + lanes

    @pl.when(i == pl.num_programs(0) - 1)
    def _():
        loss = jnp.sum(loss_ref[...], axis=(0, 1), keepdims=True)
        power = power_of(jnp.abs(loss))
        fraction = loss * jnp.exp2(-power)
        lead = fraction.astype(bf16).astype(f32)
        row = lax.broadcasted_iota(jnp.int32, (HEAD, LANES), 0)
        head = jnp.where(row == 5, tab[6, 0].astype(f32), 0.0)
        for k, part in ((2, power), (3, lead), (4, (fraction - lead) * 256.0)):
            head = jnp.where(row == k, part, head)
        at = (slice(None), pl.ds(side * width // LANES, HEAD), slice(None))
        slots_ref[at] = slots_ref[at] + head[None]


def run_blocks(table, values, a_panel, b_panel, c_panel, n_slots):
    side, width = a_panel.shape[1:]
    whole3 = lambda i, tab: (0, 0, 0)
    grid_spec = pltpu.PrefetchScalarGridSpec(
        num_scalar_prefetch=1,
        grid=(values.shape[0],),
        in_specs=[
            pl.BlockSpec((1,) + values.shape[1:], lambda i, tab: (i, 0, 0)),
            pl.BlockSpec((1, side, width), lambda i, tab: (tab[0, i], 0, 0)),
            pl.BlockSpec((1, side, width), lambda i, tab: (tab[1, i], 0, 0)),
            pl.BlockSpec((1, side, width), lambda i, tab: (tab[2, i], 0, 0)),
        ],
        out_specs=[
            pl.BlockSpec((n_slots, side * width // LANES + HEAD, LANES), whole3),
            pl.BlockSpec(b_panel.shape, whole3),
        ],
        scratch_shapes=[pltpu.VMEM((8, LANES), f32)],
    )
    return pl.pallas_call(
        block_kernel,
        out_shape=[
            jax.ShapeDtypeStruct((n_slots, side * width // LANES + HEAD, LANES), f32),
            jax.ShapeDtypeStruct(b_panel.shape, f32),
        ],
        grid_spec=grid_spec,
    )(table, values, a_panel, b_panel, c_panel)


def step(values, a_block, b_block, c_block, held, factor_a, factor_b, factor_c):
    side, width = values.shape[1], factor_a.shape[1]
    nz, nx = lax.axis_size("z"), lax.axis_size("x")
    grid_axes, wide_axes = ("y", "core"), ("z", "x")
    n_grid, n_wide = lax.axis_size(grid_axes), nz * nx
    z, x = lax.axis_index("z"), lax.axis_index("x")
    own = factor_a.shape[0] // side

    def shift(v, axis, by):
        n = lax.axis_size(axis)
        return lax.ppermute(v, axis, [(k, (k + by) % n) for k in range(n)])

    column = jnp.concatenate([factor_a] + [shift(factor_a, "z", s) for s in range(1, nz)])
    b_panel = lax.all_gather(factor_b, grid_axes, axis=0, tiled=True).reshape(-1, side, width)
    half = column.shape[0] // 2
    ahead = shift(column, "x", 1)
    back = shift(column, "x", nx - 1)
    far = [shift(ahead[:half], "x", 1), shift(back[half:], "x", nx - 1)]
    a_panel = jnp.concatenate([column, ahead, *far, back]).reshape(-1, side, width)
    c_panel = factor_c.reshape(-1, side, width)

    holder = a_block // own
    within = a_block % own
    s = (z - holder // nx) % nz
    q = (x - holder % nx) % nx
    held_count = jnp.full_like(held, jnp.sum(held))
    table = jnp.stack([(q * nz + s) * own + within, b_block, c_block, held, holder, within, held_count])
    slots, b_grad = run_blocks(table, values, a_panel, b_panel, c_panel, n_wide)

    tall = side * width // LANES
    packed, b_grad = lax.optimization_barrier((slots.astype(f16), b_grad))
    got = lax.all_to_all(packed, wide_axes, 0, 0, tiled=True)
    parts = b_grad.reshape(n_grid, -1, width)
    me = lax.axis_index(grid_axes)
    grad_b = lax.dynamic_index_in_dim(parts, me, 0, keepdims=False)
    for by in range(1, n_grid):
        part = lax.dynamic_index_in_dim(parts, (me + by) % n_grid, 0, keepdims=False)
        grad_b = grad_b + shift(part, grid_axes, by)
    heads = got[:, tall : tall + 6, 0].astype(f32)
    which, scale = heads[:, 0], jnp.exp2(heads[:, 1] - TOP)
    picked = jnp.where(which[None, :] == jnp.arange(own, dtype=f32)[:, None], scale[None, :], 0.0)
    grads = got[:, :tall].astype(f32)
    grad_a = jnp.stack([jnp.sum(picked[k][:, None, None] * grads, axis=0) for k in range(own)])
    grad_a = grad_a.reshape(own, width // LANES, side, LANES).transpose(0, 2, 1, 3)
    grad_a = grad_a.reshape(own * side, width)
    loss = jnp.sum(jnp.exp2(heads[:, 2]) * (heads[:, 3] + heads[:, 4] / 256.0))
    totals = jnp.concatenate([jnp.full((4, LANES), loss), jnp.full((4, LANES), jnp.sum(heads[:, 5]))])
    totals = jnp.broadcast_to(totals[None], (n_grid, 8, LANES))
    totals = jnp.sum(lax.all_to_all(totals, grid_axes, 0, 0, tiled=True), axis=0)[::4, 0]
    held_loss = totals[0] / (totals[1] * (side * side * side))
    next_a = factor_a.astype(f32) - step_size * grad_a
    next_b = factor_b.astype(f32) - step_size * grad_b
    return next_a, next_b, held_loss


def solution(mesh):
    fine = Mesh(mesh.devices.reshape(4, 2, 8, 4), ("y", "core", "z", "x"))
    blocks = ("y", "core", "z", "x")
    rows_b = ("z", "x", "y", "core")
    in_specs = (
        P(blocks, None, None), P(blocks), P(blocks), P(blocks), P(blocks),
        P(blocks, None), P(rows_b, None), P(),
    )
    out_specs = (P(blocks, None), P(rows_b, None), P())
    return jax.shard_map(step, mesh=fine, in_specs=in_specs, out_specs=out_specs, check_vma=False)
```
